32 devices in a mesh: dp: 8 (over z, x), expert: 4 (over y, core).
Axes of the slice: x: 2, y: 2, z: 4, core: 2. Of those that a mesh axis runs over, the one named last changes fastest.
Arguments:
- tokens: bfloat16 [2, 8, 256, 1024], P(None, 'dp', 'expert'), may hold values from -6 to 6
- out_grad: bfloat16 [2, 8, 256, 1024], P(None, 'dp', 'expert'), may hold values from -6 to 6
- routes: int32 [2, 8, 256, 8], P(None, 'dp', 'expert'), may hold values from 0 to 15, as said below
- positions: int32 [2, 8, 256], P(None, 'dp', 'expert'), may hold values from 0 to 255, as said below
- capacity: int32 [16], replicated, may hold values from 16 to 32, as said below
- norm_one: float32 [1024], replicated, may hold values from 0.25 to 1.75
- norm_two: float32 [1024], replicated, may hold values from 0.25 to 1.75
- w_query: bfloat16 [1024, 1024], replicated, may hold values from -0.1875 to 0.1875
- w_key: bfloat16 [1024, 512], replicated, may hold values from -0.1875 to 0.1875
- w_value: bfloat16 [1024, 512], replicated, may hold values from -0.1875 to 0.1875
- w_out: bfloat16 [1024, 1024], replicated, may hold values from -0.75 to 0.75
- w_router: bfloat16 [1024, 16], replicated, may hold values from -0.1875 to 0.1875
- w_gate: bfloat16 [16, 1024, 512], P('expert'), may hold values from -0.1875 to 0.1875
- w_up: bfloat16 [16, 1024, 512], P('expert'), may hold values from -0.1875 to 0.1875
- w_down: bfloat16 [16, 512, 1024], P('expert'), may hold values from -0.25 to 0.25
Outputs:
- output: bfloat16 [2, 8, 256, 1024], P(None, 'dp', 'expert')
- input_grad: bfloat16 [2, 8, 256, 1024], P(None, 'dp', 'expert')
- norm_one_grad: float32 [1024], P(('dp', 'expert'))
- norm_two_grad: float32 [1024], P(('dp', 'expert'))
- query_grad: float32 [1024, 1024], P(('dp', 'expert'))
- key_grad: float32 [1024, 512], P(('dp', 'expert'))
- value_grad: float32 [1024, 512], P(('dp', 'expert'))
- out_weight_grad: float32 [1024, 1024], P(('dp', 'expert'))
- router_grad: float32 [1024, 16], P(('dp', 'expert'))
- gate_grad: float32 [16, 1024, 512], P('expert', 'dp')
- up_grad: float32 [16, 1024, 512], P('expert', 'dp')
- down_grad: float32 [16, 512, 1024], P('expert', 'dp')
The draws below stay inside these ranges and needn't reach their ends.
Inputs may be any that keep to these rules, and one draw needn't show every extreme that they name: `routes`: each token names 8 different experts. `positions`: a token's position counts the tokens before it in its document, which lies whole in one sequence; every sequence starts a document at its first token; the first sequence of the first micro-batch is one document. The largest capacity is 32 and the smallest 32 // 2.
All inputs are finite; a program needn't handle non-finite values.
Results may differ from the reference program's by a relative error of at most 0.013.
The reference program's roundings to bfloat16 on the way count: a program that leaves them out, or rounds other values in their place, can miss the bound.
Values may be sent and summed in bfloat16 or wider, within the bound.
No kernel may reach another device: no remote copies, remote signals or barrier semaphores. Data moves between devices by JAX's collectives and lax.ppermute only.
A program may use at most 192 MiB of HBM per device.

```python
import math
import jax
import jax.numpy as jnp
from jax import lax

D = 1024
HEADS = 16
KV_HEADS = 8
HEAD_DIM = 64
FFE = 512
TOP = 8
MICRO = 2
TOK_DEV = 64
EXPERTS = 16
SEQ_LEN = 256
SEQS = 8
CAP = 32


def expert_order(key):
    return jax.random.permutation(jax.random.fold_in(key, 11), EXPERTS)


def draw_routes(key, part):
    order = expert_order(key)
    rank_of = jnp.zeros((EXPERTS,), jnp.int32).at[order].set(jnp.arange(EXPERTS, dtype=jnp.int32))
    pick_weight = (4096 // (rank_of + 3)).astype(jnp.int32)
    grid_shape = (MICRO, SEQS, SEQ_LEN, EXPERTS)
    raw_scores = jax.random.randint(jax.random.fold_in(key, 12), grid_shape, 0, pick_weight)
    distinct = raw_scores * EXPERTS + jnp.arange(EXPERTS, dtype=jnp.int32)
    _, picked = lax.top_k(distinct, TOP)
    return picked.astype(jnp.int32)


def draw_capacity(key, part):
    order = expert_order(key)
    limits = jax.random.randint(jax.random.fold_in(key, 13), (EXPERTS,), CAP // 2, CAP + 1)
    limits = limits.at[order[0]].set(CAP)
    limits = limits.at[order[EXPERTS - 1]].set(CAP // 2)
    return limits.astype(jnp.int32)


def draw_positions(key, part):
    grid_shape = (MICRO, SEQS, SEQ_LEN)
    index_grid = lax.broadcasted_iota(jnp.int32, grid_shape, 2)
    micro_grid = lax.broadcasted_iota(jnp.int32, grid_shape, 0)
    seq_grid = lax.broadcasted_iota(jnp.int32, grid_shape, 1)
    whole_doc = (micro_grid == 0) & (seq_grid == 0)
    random_starts = jax.random.randint(jax.random.fold_in(key, 14), grid_shape, 0, SEQ_LEN) < 3
    starts = random_starts & jnp.logical_not(whole_doc) | (index_grid == 0)
    first_start = lax.cummax(jnp.where(starts, index_grid, 0), axis=2)
    return (index_grid - first_start).astype(jnp.int32)


def raised(values, rng, source, target, parts, factor):
    def block_of(axis_at):
        return (jnp.arange(values.shape[axis_at]) // (values.shape[axis_at] // parts)).reshape((-1,) + (1,) * (values.ndim - 1 - axis_at))

    first = jax.random.permutation(rng, parts)[block_of(target)]
    far = (block_of(target) + parts // 2) % parts
    return jnp.where((block_of(source) == first) | (block_of(source) == far), factor * values, values)


def block_levels(stream_key, shape, pieces, least, high):
    def one(axis_at, shards_of):
        draws = jax.random.uniform(jax.random.fold_in(jax.random.fold_in(stream_key, 6), axis_at), (shards_of,), jnp.float32, least / len(pieces), high / len(pieces))
        return jnp.repeat(jnp.exp(draws), shape[axis_at] // shards_of).reshape((-1,) + (1,) * (len(shape) - axis_at - 1))

    factor_of = one(*pieces[0])
    for cut in pieces[1:]:
        factor_of = factor_of * one(*cut)
    return factor_of


def scatter_about(own_key, dims, deviation, reach, split=(), kind=jnp.bfloat16):
    gain = block_levels(own_key, dims, split, -0.22, 0.18) if split else 1.0
    values = jax.random.normal(own_key, dims, jnp.float32) * deviation * gain
    return jnp.minimum(jnp.maximum(values, -reach), reach).astype(kind)


def heavy_noise(stream_key, dims, width, reach, split, heavy, held_as=jnp.bfloat16):
    entries = width * jax.random.normal(stream_key, dims, jnp.float32)
    if split:
        entries = entries * block_levels(stream_key, dims, split, -0.22, 0.18)
    return jnp.clip(raised(entries, jax.random.fold_in(stream_key, 3), *heavy), -reach, reach).astype(held_as)


def setup_inputs(seed: int = 0) -> dict:
    arg_keys = jax.random.split(jax.random.key(seed), 16)
    tokens = heavy_noise(arg_keys[0], (MICRO, SEQS, SEQ_LEN, D), 1.0, 6.0, ((1, 8), (2, 4)), (1, 3, 8, 2.0))
    out_grad = scatter_about(arg_keys[1], (MICRO, SEQS, SEQ_LEN, D), 1.0, 6.0, ((1, 8), (2, 4)))
    routes = draw_routes(jax.random.fold_in(arg_keys[15], 71), 0)
    positions = draw_positions(jax.random.fold_in(arg_keys[15], 71), 0)
    capacity = draw_capacity(jax.random.fold_in(arg_keys[15], 71), 0)
    norm_one = jnp.clip(1.0 + 0.15 * jax.random.normal(arg_keys[5], (D,), jnp.float32), 0.25, 1.75)
    norm_two = jnp.clip(1.0 + 0.15 * jax.random.normal(arg_keys[6], (D,), jnp.float32), 0.25, 1.75)
    w_query = scatter_about(arg_keys[7], (D, D), D ** -0.5, 0.1875)
    w_key = scatter_about(arg_keys[8], (D, KV_HEADS * HEAD_DIM), D ** -0.5, 0.1875)
    w_value = scatter_about(arg_keys[9], (D, KV_HEADS * HEAD_DIM), D ** -0.5, 0.1875)
    w_out = scatter_about(arg_keys[10], (D, D), HEAD_DIM ** -0.5, 0.75)
    w_router = scatter_about(arg_keys[11], (D, EXPERTS), D ** -0.5, 0.1875)
    w_gate = scatter_about(arg_keys[12], (EXPERTS, D, FFE), D ** -0.5, 0.1875, ((0, 4),))
    w_up = scatter_about(arg_keys[13], (EXPERTS, D, FFE), D ** -0.5, 0.1875, ((0, 4),))
    w_down = scatter_about(arg_keys[14], (EXPERTS, FFE, D), FFE ** -0.5, 0.25, ((0, 4),))
    return dict(tokens=tokens, out_grad=out_grad, routes=routes, positions=positions, capacity=capacity, norm_one=norm_one, norm_two=norm_two, w_query=w_query, w_key=w_key, w_value=w_value, w_out=w_out, w_router=w_router, w_gate=w_gate, w_up=w_up, w_down=w_down)


@jax.custom_vjp
def low(v):
    return lax.optimization_barrier(v.astype(jnp.bfloat16)).astype(jnp.float32)

@jax.custom_vjp
def low_back(v):
    return v

def low_keep(v):
    return (low(v), None)

def low_pass(kept, grad):
    return (grad,)

def back_keep(v):
    return (v, None)

def back_low(kept, grad):
    return (low(grad),)
low.defvjp(low_keep, low_pass)
low_back.defvjp(back_keep, back_low)
epsilon = 1e-06
rope_base = 10000.0
masked_score = -1e+30
highest = lax.Precision.HIGHEST

def rms_scale(values, gain_row):
    return values * lax.rsqrt(lax.optimization_barrier(jnp.mean(values * values, axis=-1, keepdims=True)) + epsilon) * gain_row

def rope_tables(positions):
    half_dim = HEAD_DIM // 2
    inverse_freq = jnp.exp(-jnp.log(rope_base) * jnp.arange(half_dim, dtype=jnp.float32) * 2.0 / HEAD_DIM)
    angles = positions.astype(jnp.float32)[:, None] * inverse_freq[None, :]
    return (jnp.cos(angles)[:, None, :], jnp.sin(angles)[:, None, :])

def rotate(values, cos_table, sin_table, direction):
    half_dim = values.shape[-1] // 2
    first_half = values[..., :half_dim]
    second_half = values[..., half_dim:]
    return jnp.concatenate([first_half * cos_table - direction * second_half * sin_table, second_half * cos_table + direction * first_half * sin_table], axis=-1)

def route_slots(route_ids, capacity):
    tok_count = route_ids.shape[0]
    expert_ids = jnp.arange(EXPERTS, dtype=jnp.int32)
    route_hits = (route_ids[:, :, None] == expert_ids[None, None, :]).astype(jnp.int32)
    per_expert = lax.optimization_barrier(jnp.sum(route_hits, axis=1)).astype(jnp.int32)
    earlier = (jnp.cumsum(per_expert, axis=0) - per_expert).astype(jnp.int32)
    pair_rank = lax.optimization_barrier(jnp.sum(route_hits * earlier[:, None, :], axis=2)).astype(jnp.int32)
    pair_limit = lax.optimization_barrier(jnp.sum(route_hits * capacity[None, None, :], axis=2)).astype(jnp.int32)
    empty_slot = EXPERTS * CAP
    pair_slot = jnp.where(pair_rank < pair_limit, route_ids * CAP + pair_rank, empty_slot).astype(jnp.int32)
    owners = jnp.repeat(jnp.arange(tok_count, dtype=jnp.int32), route_ids.shape[1])
    slot_token = jnp.full((empty_slot,), tok_count, jnp.int32).at[pair_slot.reshape(-1)].set(owners, mode='drop')
    return (pair_slot, slot_token)

def take_rows(source, indices):
    return source[indices]

def one_sequence(weights, inputs, route_ids, positions, capacity):
    norm_one, norm_two, w_query, w_key, w_value, w_out, w_router, w_gate, w_up, w_down = weights
    seq_rows = inputs.shape[0]
    group_size = HEADS // KV_HEADS
    normed = low(rms_scale(inputs, norm_one))
    query_raw = low_back(jnp.dot(normed, w_query, precision=highest))
    key_raw = low_back(jnp.dot(normed, w_key, precision=highest))
    value_rows = low(low_back(jnp.dot(normed, w_value, precision=highest))).reshape(seq_rows, KV_HEADS, HEAD_DIM)
    cos_table, sin_table = rope_tables(positions)
    queries = low(rotate(query_raw.reshape(seq_rows, HEADS, HEAD_DIM), cos_table, sin_table, 1.0))
    queries = queries.reshape(seq_rows, KV_HEADS, group_size, HEAD_DIM)
    key_rows = low(rotate(key_raw.reshape(seq_rows, KV_HEADS, HEAD_DIM), cos_table, sin_table, 1.0))
    scores = low_back(jnp.einsum('qhgd,khd->hgqk', queries, key_rows, precision=highest) * (1.0 / math.sqrt(HEAD_DIM)))
    index_rows = jnp.arange(seq_rows, dtype=jnp.int32)
    allowed = (index_rows[None, :] <= index_rows[:, None]) & (index_rows[None, :] >= (index_rows - positions)[:, None])
    scores = jnp.where(allowed, scores, masked_score)
    attn_probs = jax.nn.softmax(scores, axis=-1)
    mixed_rows = jnp.einsum('hgqk,khd->qhgd', low(attn_probs), value_rows, precision=highest).reshape(seq_rows, D)
    mixed_rows = low(low_back(mixed_rows))
    hidden = inputs + low_back(jnp.dot(mixed_rows, w_out, precision=highest))
    normed_two = low(rms_scale(hidden, norm_two))
    logits = low_back(jnp.dot(normed_two, w_router, precision=highest))
    gate_probs = jax.nn.softmax(jnp.take_along_axis(logits, route_ids, axis=1), axis=-1)
    blocks = seq_rows // TOK_DEV
    pair_slot, slot_token = jax.vmap(route_slots, in_axes=(0, None))(route_ids.reshape(blocks, TOK_DEV, TOP), capacity)
    block_rows = normed_two.reshape(blocks, TOK_DEV, D)
    padded_rows = jnp.concatenate([block_rows, jnp.zeros((blocks, 1, D), jnp.float32)], axis=1)
    expert_rows = low_back(jax.vmap(take_rows)(padded_rows, slot_token)).reshape(blocks, EXPERTS, CAP, D)
    gate_pre = low_back(jnp.einsum('becd,edf->becf', expert_rows, w_gate, precision=highest))
    up_pre = low_back(jnp.einsum('becd,edf->becf', expert_rows, w_up, precision=highest))
    activation = low(jax.nn.silu(gate_pre) * up_pre)
    expert_out = low(low_back(jnp.einsum('becf,efd->becd', activation, w_down, precision=highest)))
    expert_out = expert_out.reshape(blocks, EXPERTS * CAP, D)
    padded_out = jnp.concatenate([expert_out, jnp.zeros((blocks, 1, D), jnp.float32)], axis=1)
    paired = jax.vmap(take_rows)(padded_out, pair_slot)
    mixture = lax.optimization_barrier(jnp.sum(gate_probs.reshape(blocks, TOK_DEV, TOP, 1) * paired, axis=2)).reshape(seq_rows, D)
    return hidden + mixture

def reference(tokens, out_grad, routes, positions, capacity, norm_one, norm_two, w_query, w_key, w_value, w_out, w_router, w_gate, w_up, w_down):
    params = (norm_one, norm_two, w_query, w_key, w_value, w_out, w_router, w_gate, w_up, w_down)
    params = tuple((weight.astype(jnp.float32) for weight in params))
    seq_count = MICRO * SEQS
    inputs_all = tokens.astype(jnp.float32).reshape(seq_count, SEQ_LEN, D)
    route_rows = routes.reshape(seq_count, SEQ_LEN, TOP)
    position_rows = positions.reshape(seq_count, SEQ_LEN)

    def forward(weights, rows_all):

        def seq_step(state_in, seq_item):
            inputs, route_ids, token_pos = seq_item
            return (state_in, jax.checkpoint(one_sequence)(weights, inputs, route_ids, token_pos, capacity))
        _, outputs = lax.scan(seq_step, None, (rows_all, route_rows, position_rows))
        return outputs
    outputs, pullback = jax.vjp(forward, params, inputs_all)
    weight_grads, input_grad = pullback(out_grad.astype(jnp.float32).reshape(seq_count, SEQ_LEN, D))
    full_shape = (MICRO, SEQS, SEQ_LEN, D)
    return (outputs.reshape(full_shape).astype(jnp.bfloat16), input_grad.reshape(full_shape).astype(jnp.bfloat16), weight_grads[0], weight_grads[1], weight_grads[2], weight_grads[3], weight_grads[4], weight_grads[5], weight_grads[6], weight_grads[7], weight_grads[8], weight_grads[9])
```

```python
import functools
import math

import jax
import jax.numpy as jnp
from jax import lax
from jax.experimental import pallas as pl
from jax.experimental.pallas import tpu as pltpu
from jax.sharding import PartitionSpec as P

HEADS = 16
KV_HEADS = 8
HEAD_DIM = 64
TOP = 8
CAP = 32
GROUP = 4

epsilon = 1e-06
rope_base = 10000.0
masked_score = -1e30
score_scale = 1.0 / math.sqrt(HEAD_DIM)

f32 = jnp.float32
bf16 = jnp.bfloat16


def dot(a, b):
    return lax.dot_general(a, b, (((1,), (0,)), ((), ())), preferred_element_type=f32)


def dot_t(a, b):
    return lax.dot_general(a, b, (((1,), (1,)), ((), ())), preferred_element_type=f32)


def t_dot(a, b):
    return lax.dot_general(a, b, (((0,), (0,)), ((), ())), preferred_element_type=f32)


def lanes(shape):
    return lax.broadcasted_iota(jnp.int32, shape, len(shape) - 1)


def subs(shape):
    return lax.broadcasted_iota(jnp.int32, shape, len(shape) - 2)


def swap_halves(v):
    width = v.shape[-1]
    half = HEAD_DIM // 2
    first = lanes(v.shape) % HEAD_DIM < half
    return jnp.where(first, pltpu.roll(v, width - half, 1), pltpu.roll(v, half, 1))


def run(body, out_shapes, args, specs, scratch=(), name=None, flops=0, out_specs=None):
    nbytes = sum(math.prod(a.shape) * a.dtype.itemsize for a in args)
    vm = pl.BlockSpec(memory_space=pltpu.VMEM)
    return pl.pallas_call(
        body,
        out_shape=out_shapes,
        in_specs=specs,
        out_specs=jax.tree.map(lambda _: vm, out_shapes) if out_specs is None else out_specs,
        scratch_shapes=list(scratch),
        name=name,
        cost_estimate=pl.CostEstimate(flops=flops, bytes_accessed=nbytes, transcendentals=0),
    )(*args)


VM = pl.BlockSpec(memory_space=pltpu.VMEM)
SM = pl.BlockSpec(memory_space=pltpu.SMEM)
HB = pl.BlockSpec(memory_space=pl.ANY)


def sds(shape, dtype):
    return jax.ShapeDtypeStruct(shape, dtype)


def head_pair(v, kv):
    low = lanes(v.shape) < HEAD_DIM
    other = pltpu.roll(v.astype(f32), HEAD_DIM, 1).astype(v.dtype)
    return jnp.where(low, v, other) if kv == 0 else jnp.where(low, other, v)


def allowed_of(expert, pos, seq_rows, tok_rows):
    shape = (seq_rows, seq_rows)
    row = subs(shape)
    col = lanes(shape)
    q_index = (row // tok_rows ^ expert) * tok_rows + row % tok_rows
    k_index = (col // tok_rows ^ expert) * tok_rows + col % tok_rows
    return (k_index <= q_index) & (k_index >= q_index - pos)


def attention_kernel(
    ids, x0, x1, x2, x3, gain, tab, wq, wk, wv,
    normed, q_out, k_out, v_out, tabs_out, mixed,
    wq_s, wk_s, wv_s, sems,
):
    e = ids[0]
    width = gain.shape[1]
    qw = q_out.shape[1]
    kw = k_out.shape[1]
    tok = x0.shape[1]
    micro = x0.shape[0]
    seq = tok * GROUP
    copies = [
        pltpu.make_async_copy(wq.at[:, pl.ds(pl.multiple_of(e * qw, 128), qw)], wq_s, sems.at[0]),
        pltpu.make_async_copy(wk.at[:, pl.ds(pl.multiple_of(e * kw, 128), kw)], wk_s, sems.at[1]),
        pltpu.make_async_copy(wv.at[:, pl.ds(pl.multiple_of(e * kw, 128), kw)], wv_s, sems.at[2]),
    ]
    for c in copies:
        c.start()
    pieces = (x0, x1, x2, x3)
    positions = []
    for m in range(micro):
        for r in range(GROUP):
            rows = slice((m * GROUP + r) * tok, (m * GROUP + r + 1) * tok)
            inputs = pieces[r][m, :, :width].astype(f32)
            positions.append(pieces[r][m, :, width + TOP : width + TOP + 1].astype(f32))
            root = lax.rsqrt(jnp.mean(inputs * inputs, axis=-1, keepdims=True) + epsilon)
            normed[rows, :] = (inputs * root * gain[...]).astype(bf16)
    pos = jnp.concatenate(positions, axis=0).astype(jnp.int32)
    hot = (lanes((micro * seq, tab.shape[0])) == pos).astype(f32)
    tabs = lax.dot_general(
        hot, tab[...], (((1,), (0,)), ((), ())),
        precision=lax.Precision.HIGHEST, preferred_element_type=f32,
    )
    tabs_out[...] = tabs
    cos = tabs[:, :128]
    sin = tabs[:, 128:]
    for c in copies:
        c.wait()
    for h in range(qw // 128):
        raw = dot(normed[...], wq_s[:, h * 128 : (h + 1) * 128])
        q_out[:, h * 128 : (h + 1) * 128] = (raw * cos + swap_halves(raw) * sin).astype(bf16)
    raw = dot(normed[...], wk_s[...])
    k_out[...] = (raw * cos + swap_halves(raw) * sin).astype(bf16)
    v_out[...] = dot(normed[...], wv_s[...]).astype(bf16)
    low = lanes((seq, 128)) < HEAD_DIM
    for m in range(micro):
        rows = slice(m * seq, (m + 1) * seq)
        allowed = allowed_of(e, pos[rows], seq, tok)
        for kv in range(kw // HEAD_DIM):
            keys = head_pair(k_out[rows, :], kv)
            values = head_pair(v_out[rows, :], kv)
            q_two = q_out[rows, kv * 128 : (kv + 1) * 128]
            parts = []
            for g in range(2):
                q_one = jnp.where(low == (g == 0), q_two, jnp.zeros_like(q_two))
                scores = jnp.where(allowed, dot_t(q_one, keys) * score_scale, masked_score)
                exps = jnp.exp(scores - jnp.max(scores, axis=-1, keepdims=True))
                probs = (exps / jnp.sum(exps, axis=-1, keepdims=True)).astype(bf16)
                parts.append(dot(probs, values))
            both = jnp.where(low, parts[0], parts[1]).astype(bf16)
            for r in range(GROUP):
                mixed[r, m, :, kv * 128 : (kv + 1) * 128] = both[r * tok : (r + 1) * tok]


def route_kernel(
    ids, x0, x1, x2, x3, m0, m1, m2, m3, g0, g1, g2, g3, gain, w_router, cap, w_out,
    hidden_own, nt, gall, gates_out, tgt_out, gates_t, tgt_t,
    wo_s, sems,
):
    e = ids[0]
    micro, tok, _ = x0.shape
    width = gain.shape[1]
    hw = m0.shape[3]
    copies = []
    for r in range(GROUP):
        start = pl.multiple_of((e ^ r) * hw, 128)
        copies.append(pltpu.make_async_copy(w_out.at[pl.ds(start, hw), :], wo_s.at[r], sems.at[r]))
        copies[-1].start()
    xs = (x0, x1, x2, x3)
    gs = (g0, g1, g2, g3)
    ms = (m0, m1, m2, m3)
    expert_lane = lanes((tok, 128))
    below = (subs((tok, tok)) > lanes((tok, tok))).astype(bf16)
    for m in range(micro):
        for b in range(GROUP):
            rows = slice((m * GROUP + b) * tok, (m * GROUP + b + 1) * tok)
            gall[rows, :] = gs[b][m]
    for c in copies:
        c.wait()
    for m in range(micro):
        blocks = []
        for r in range(GROUP):
            mine = jnp.concatenate([ms[r][b ^ r, m] for b in range(GROUP)], axis=0)
            blocks.append(dot(mine, wo_s[r]))
        branch = (blocks[0] + blocks[1]) + (blocks[2] + blocks[3])
        for b in range(GROUP):
            block = m * GROUP + b
            rows = slice(block * tok, (block + 1) * tok)
            hidden = xs[b][m, :, :width].astype(f32) + branch[b * tok : (b + 1) * tok]
            if b == 0:
                hidden_own[m] = hidden
            root = lax.rsqrt(jnp.mean(hidden * hidden, axis=-1, keepdims=True) + epsilon)
            low = (hidden * root * gain[...]).astype(bf16)
            nt[rows, :] = low
            logits = dot(low, w_router[...])
            named = xs[b][m, :, width : width + 128].astype(jnp.int32)
            hits = expert_lane == named[:, 0:1]
            for k in range(1, TOP):
                hits = hits | (expert_lane == named[:, k : k + 1])
            earlier = dot(below, hits.astype(bf16))
            kept = hits & (earlier < cap[...])
            chosen = jnp.where(hits, logits, masked_score)
            exps = jnp.where(hits, jnp.exp(chosen - jnp.max(chosen, axis=-1, keepdims=True)), 0.0)
            gates_out[rows, :] = exps / jnp.sum(exps, axis=-1, keepdims=True)
            tgt_out[rows, :] = jnp.where(kept, earlier + float(block * CAP), -1.0)
    gates_t[...] = jnp.transpose(gates_out[...])[: gates_t.shape[0]]
    tgt_t[...] = jnp.transpose(tgt_out[...])[: tgt_t.shape[0]]


def relative_order(count, order):
    places = []
    for p in range(count):
        rel = 0
        for stage, bit in enumerate(order):
            if p >> (len(order) - 1 - stage) & 1:
                rel |= bit
        places.append(rel)
    return places


def expert_kernel(
    j, order, ids, nt, gall, gates_t, tgt_t, w_gate, w_up, w_down,
    send, keep, eo_out, rg_out, pgg_out,
    wg_s, wu_s, wd_s, d_one, d_two, d_three, sems,
):
    e, d = ids[0], ids[1]
    copies = [
        pltpu.make_async_copy(w_gate.at[j], wg_s, sems.at[0]),
        pltpu.make_async_copy(w_up.at[j], wu_s, sems.at[1]),
        pltpu.make_async_copy(w_down.at[j], wd_s, sems.at[2]),
    ]
    for c in copies:
        c.start()
    tokens = nt.shape[0]
    slots = eo_out.shape[0]
    local = w_gate.shape[0]
    tgt = tgt_t[pl.ds(e * local + j, 1), :].astype(jnp.int32)
    gate = gates_t[pl.ds(e * local + j, 1), :]
    here = subs((slots, tokens)) == tgt
    pick = here.astype(bf16)
    rows = dot(pick, nt[...]).astype(bf16)
    g_rows = dot(pick, gall[...])
    slot_gate = jnp.sum(jnp.where(here, gate, 0.0), axis=1, keepdims=True)
    slot_grad = (g_rows * slot_gate).astype(bf16)
    for c in copies:
        c.wait()
    gate_pre = dot(rows, wg_s[...])
    up_pre = dot(rows, wu_s[...])
    sig = 1.0 / (1.0 + jnp.exp(-gate_pre))
    silu = gate_pre * sig
    act = (silu * up_pre).astype(bf16)
    eo = dot(act, wd_s[...]).astype(bf16)
    eo_out[...] = eo
    pair = jnp.sum(g_rows * eo.astype(f32), axis=1, keepdims=True)
    pgg_out[...] = jnp.broadcast_to(
        jnp.sum(jnp.where(here, pair, 0.0), axis=0, keepdims=True), pgg_out.shape
    )
    act_grad = dot_t(slot_grad, wd_s[...])
    gpg = (act_grad * up_pre * sig * (1.0 + gate_pre * (1.0 - sig))).astype(bf16)
    upg = (act_grad * silu).astype(bf16)
    rg_out[...] = (dot_t(gpg, wg_s[...]) + dot_t(upg, wu_s[...])).astype(bf16)
    d_one[...] = t_dot(rows, gpg)
    d_two[...] = t_dot(rows, upg)
    d_three[...] = t_dot(act, slot_grad)
    half = send.shape[0]
    cols = send.shape[2]
    dp = 2 * half
    big = d_one.shape[0] // dp
    small = d_three.shape[0] // dp
    for p, rel in enumerate(order):
        out = (send if p >= half else keep).at[p % half]
        at = d ^ rel
        one = pl.ds(pl.multiple_of(at * big, 8), big)
        three = pl.ds(pl.multiple_of(at * small, 8), small)
        out[0:big, :] = d_one[one, :].astype(bf16)
        out[big : 2 * big, :] = d_two[one, :].astype(bf16)
        out[2 * big : 2 * big + small, :] = d_three[three, :cols].astype(bf16)
        out[2 * big + small : 2 * big + 2 * small, :] = d_three[three, cols:].astype(bf16)


def combine_kernel(
    ids, gates, tgt, e0, e1, e2, e3, r0, r1, r2, r3, p0, p1, p2, p3,
    rg0, rg2, rg_send, mix0, mix2, mix_send, pair_s,
):
    e = ids[0]
    outs = (e0, e1, e2, e3)
    grads = (r0, r1, r2, r3)
    pairs = (p0, p1, p2, p3)
    micro, tok, width = mix0.shape
    slots = e0.shape[0]
    local = len(outs)
    pair_s[...] = jnp.zeros_like(pair_s)
    for j in range(local):
        pair_s[pl.ds(e * local + j, 1), :] = pairs[j][0:1, :]
    pair = jnp.transpose(pair_s[...])
    high = pair.astype(bf16)
    low = (pair - high.astype(f32)).astype(bf16)
    both = high.astype(f32) + pltpu.roll(low.astype(f32), 16, 1)
    for m in range(micro):
        for b in range(GROUP):
            block = m * GROUP + b
            rows = slice(block * tok, (block + 1) * tok)
            lane = lanes((tok, 128))
            mix = None
            grad = None
            for j in range(local):
                mine = lane == e * local + j
                where = jnp.sum(jnp.where(mine, tgt[rows, :], 0.0), axis=1, keepdims=True)
                gate = jnp.sum(jnp.where(mine, gates[rows, :], 0.0), axis=1, keepdims=True)
                pick = (lanes((tok, slots)) == where.astype(jnp.int32)).astype(bf16)
                term = gate * dot(pick, outs[j][...])
                back = dot(pick, grads[j][...])
                mix = term if mix is None else mix + term
                grad = back if grad is None else grad + back
            mix = mix.astype(bf16)
            grad = grad.astype(bf16)
            extra = both[rows].astype(bf16)
            if b % 2:
                mix_send[b // 2, m] = mix
                target = rg_send.at[b // 2, m]
            else:
                (mix0 if b == 0 else mix2)[m] = mix
                target = (rg0 if b == 0 else rg2).at[m]
            target[:, :width] = grad
            target[:, width:] = extra


def hidden_kernel(
    ids, rg0, rc, ry, hidden_own, nt, gates, g0, gain, w_router,
    hidden_grad, branch_grad, small,
):
    micro, tok, width = hidden_own.shape
    total_two = jnp.zeros((1, width), f32)
    total_router = jnp.zeros((128, width), f32)
    for m in range(micro):
        rows = slice(m * GROUP * tok, (m * GROUP + 1) * tok)
        summed = rg0[m].astype(f32) + rc[0, m].astype(f32) + ry[m].astype(f32)
        extra = summed[:, width:]
        pair = extra + pltpu.roll(extra, 112, 1)
        gate = gates[rows, :]
        inner = jnp.sum(gate * pair, axis=-1, keepdims=True)
        logit_grad = (gate * (pair - inner)).astype(bf16)
        grad = summed[:, :width] + dot_t(logit_grad, w_router[...])
        hidden = hidden_own[m]
        root = lax.rsqrt(jnp.mean(hidden * hidden, axis=-1, keepdims=True) + epsilon)
        weighted = grad * gain[...]
        mean = jnp.mean(weighted * hidden, axis=-1, keepdims=True)
        out = g0[m].astype(f32) + root * weighted - hidden * (root * root * root) * mean
        hidden_grad[m] = out
        branch_grad[m] = out.astype(bf16)
        total_two = total_two + jnp.sum(grad * hidden * root, axis=0, keepdims=True)
        total_router = total_router + t_dot(logit_grad, nt[rows, :])
    small[0:16, :] = total_router[0:16]
    small[16:17, :] = total_two
    small[17:, :] = jnp.zeros_like(small[17:, :])


def backward_kernel(
    order, ids, x0, x1, x2, x3, m0, m1, m2, m3, b0, b1, b2, b3,
    normed, q_in, k_in, v_in, tabs, gain, small, wq, wk, wv, w_out,
    send, keep, ng0, ng2, ng_send,
    bg, mg, pre, wq_s, wk_s, wv_s, wo_s, dense, small_s, sems,
):
    e, d = ids[0], ids[1]
    width = gain.shape[1]
    qw = q_in.shape[1]
    kw = k_in.shape[1]
    micro, tok, _ = x0.shape
    seq = tok * GROUP
    copies = [
        pltpu.make_async_copy(w_out.at[pl.ds(pl.multiple_of(e * qw, 128), qw), :], wo_s, sems.at[3]),
        pltpu.make_async_copy(wq.at[:, pl.ds(pl.multiple_of(e * qw, 128), qw)], wq_s, sems.at[0]),
        pltpu.make_async_copy(wk.at[:, pl.ds(pl.multiple_of(e * kw, 128), kw)], wk_s, sems.at[1]),
        pltpu.make_async_copy(wv.at[:, pl.ds(pl.multiple_of(e * kw, 128), kw)], wv_s, sems.at[2]),
    ]
    for c in copies:
        c.start()
    xs = (x0, x1, x2, x3)
    ms = (m0, m1, m2, m3)
    bs = (b0, b1, b2, b3)
    for m in range(micro):
        for r in range(GROUP):
            bg[(m * GROUP + r) * tok : (m * GROUP + r + 1) * tok, :] = bs[r][m]
    copies[0].wait()
    mg[...] = dot_t(bg[...], wo_s[...]).astype(bf16)
    low = lanes((seq, 128)) < HEAD_DIM
    for m in range(micro):
        rows = slice(m * seq, (m + 1) * seq)
        pos = jnp.concatenate(
            [xs[r][m, :, width + TOP : width + TOP + 1].astype(f32) for r in range(GROUP)], axis=0
        ).astype(jnp.int32)
        allowed = allowed_of(e, pos, seq, tok)
        cos = tabs[rows, :128]
        sin = tabs[rows, 128:]
        key_parts = []
        value_parts = []
        for kv in range(kw // HEAD_DIM):
            keys = head_pair(k_in[rows, :], kv)
            values = head_pair(v_in[rows, :], kv)
            q_two = q_in[rows, kv * 128 : (kv + 1) * 128]
            g_two = mg[rows, kv * 128 : (kv + 1) * 128]
            q_parts = []
            d_key = None
            d_value = None
            for g in range(2):
                q_one = jnp.where(low == (g == 0), q_two, jnp.zeros_like(q_two))
                g_one = jnp.where(low == (g == 0), g_two, jnp.zeros_like(g_two))
                scores = jnp.where(allowed, dot_t(q_one, keys) * score_scale, masked_score)
                exps = jnp.exp(scores - jnp.max(scores, axis=-1, keepdims=True))
                probs = exps / jnp.sum(exps, axis=-1, keepdims=True)
                prob_grad = dot_t(g_one, values)
                inner = jnp.sum(probs * prob_grad, axis=-1, keepdims=True)
                score_grad = (probs * (prob_grad - inner)).astype(bf16)
                q_parts.append(dot(score_grad, keys))
                key_term = t_dot(score_grad, q_one)
                value_term = t_dot(probs.astype(bf16), g_one)
                d_key = key_term if d_key is None else d_key + key_term
                d_value = value_term if d_value is None else d_value + value_term
            d_query = jnp.where(low, q_parts[0], q_parts[1]) * score_scale
            pre[rows, kv * 128 : (kv + 1) * 128] = (
                d_query * cos - swap_halves(d_query) * sin
            ).astype(bf16)
            key_parts.append(d_key + pltpu.roll(d_key, HEAD_DIM, 1))
            value_parts.append(d_value + pltpu.roll(d_value, HEAD_DIM, 1))
        d_key = jnp.where(low, key_parts[0], key_parts[1]) * score_scale
        pre[rows, qw : qw + kw] = (d_key * cos - swap_halves(d_key) * sin).astype(bf16)
        pre[rows, qw + kw : qw + 2 * kw] = jnp.where(low, value_parts[0], value_parts[1]).astype(bf16)
    for c in copies[1:]:
        c.wait()
    total = jnp.zeros((1, width), f32)
    for m in range(micro):
        for b in range(GROUP):
            rows = slice((m * GROUP + b) * tok, (m * GROUP + b + 1) * tok)
            grad = (
                dot_t(pre[rows, :qw], wq_s[...])
                + dot_t(pre[rows, qw : qw + kw], wk_s[...])
                + dot_t(pre[rows, qw + kw :], wv_s[...])
            )
            inputs = xs[b][m, :, :width].astype(f32)
            root = lax.rsqrt(jnp.mean(inputs * inputs, axis=-1, keepdims=True) + epsilon)
            total = total + jnp.sum(grad * inputs * root, axis=0, keepdims=True)
            grad = grad.astype(bf16)
            if b % 2:
                ng_send[b // 2, m] = grad
            else:
                (ng0 if b == 0 else ng2)[m] = grad
    dw = qw + 2 * kw
    dense[:, :dw] = t_dot(normed[...], pre[...])
    own = bg[:, pl.ds(pl.multiple_of(e * qw, 128), qw)]
    for r in range(GROUP):
        mine = jnp.concatenate(
            [ms[r][b ^ r, m] for m in range(micro) for b in range(GROUP)], axis=0
        )
        dense[pl.ds(pl.multiple_of((e ^ r) * qw, 8), qw), dw : dw + qw] = t_dot(mine, own)
    small_s[...] = jnp.zeros_like(small_s)
    small_s[0 : small.shape[0], :] = small[...]
    small_s[17:18, :] = total
    dense[:, dw + qw :] = jnp.transpose(small_s[...])
    half = send.shape[0]
    big = dense.shape[0] // (2 * half)
    for p, rel in enumerate(order):
        out = (send if p >= half else keep).at[p % half]
        out[...] = dense[pl.ds(pl.multiple_of((d ^ rel) * big, 8), big), :].astype(bf16)


def final_kernel(
    x0, ng0, nc, ny, hidden_grad, gain, hidden_own, mix0, mc, my, out, input_grad
):
    micro, tok, width = ng0.shape
    for m in range(micro):
        inputs = x0[m, :, :width].astype(f32)
        root = lax.rsqrt(jnp.mean(inputs * inputs, axis=-1, keepdims=True) + epsilon)
        grad = ng0[m].astype(f32) + nc[0, m].astype(f32) + ny[m].astype(f32)
        weighted = grad * gain[...]
        mean = jnp.mean(weighted * inputs, axis=-1, keepdims=True)
        part = root * weighted - inputs * (root * root * root) * mean
        input_grad[m] = (hidden_grad[m] + part).astype(bf16)
        mixture = mix0[m].astype(f32) + mc[0, m].astype(f32) + my[m].astype(f32)
        out[m] = (hidden_own[m] + mixture).astype(bf16)


def on_device(
    tokens,
    out_grad,
    routes,
    positions,
    capacity,
    norm_one,
    norm_two,
    w_query,
    w_key,
    w_value,
    w_out,
    w_router,
    w_gate,
    w_up,
    w_down,
):
    micro, _, tok, width = tokens.shape
    dp = lax.axis_size("dp")
    assert lax.axis_size("expert") == GROUP and dp & (dp - 1) == 0
    local = w_gate.shape[0]
    experts = local * GROUP
    hidden_units = w_gate.shape[2]
    total = micro * GROUP * tok
    qw = HEADS * HEAD_DIM // GROUP
    kw = KV_HEADS * HEAD_DIM // GROUP
    slots = micro * GROUP * CAP

    def swap(x, bit, axis="expert"):
        n = lax.axis_size(axis)
        return lax.ppermute(x, axis, [(i, i ^ bit) for i in range(n)])

    def gather(x):
        far = swap(x, 2)
        near = swap(x, 1)
        return (x, near, far, swap(far, 1))

    def scatter_sum(own, far, send):
        got = swap(send, 1)
        return got, swap((far.astype(f32) + got[1].astype(f32)).astype(bf16), 2)

    ids = jnp.stack([lax.axis_index("expert"), lax.axis_index("dp")]).astype(jnp.int32)
    gain_one = norm_one[None, :]
    gain_two = norm_two[None, :]
    meta = jnp.concatenate(
        [
            routes[:, 0].astype(bf16),
            positions[:, 0, :, None].astype(bf16),
            jnp.zeros((micro, tok, 128 - TOP - 1), bf16),
        ],
        axis=-1,
    )
    xs = gather(jnp.concatenate([tokens[:, 0], meta], axis=-1))
    g_own = out_grad[:, 0]
    gs = gather(g_own)
    half_dim = HEAD_DIM // 2
    inverse_freq = jnp.exp(
        -jnp.log(rope_base) * jnp.arange(half_dim, dtype=f32) * 2.0 / HEAD_DIM
    )
    seq = tok * GROUP
    angles = jnp.arange(seq, dtype=f32)[:, None] * inverse_freq[None, :]
    cos, sin = jnp.cos(angles), jnp.sin(angles)
    tab = jnp.concatenate([cos] * 4 + [-sin, sin] * 2, axis=-1)
    router_pad = jnp.pad(w_router, ((0, 0), (0, 128 - experts)))
    cap_pad = jnp.pad(capacity.astype(f32), (0, 128 - experts))[None, :]

    normed, q, k, v, tabs, mixed = run(
        attention_kernel,
        (
            sds((total, width), bf16),
            sds((total, qw), bf16),
            sds((total, kw), bf16),
            sds((total, kw), bf16),
            sds((total, 256), f32),
            sds((GROUP, micro, tok, qw), bf16),
        ),
        (ids, *xs, gain_one, tab, w_query, w_key, w_value),
        [SM] + [VM] * 6 + [HB] * 3,
        scratch=[
            pltpu.VMEM((width, qw), bf16),
            pltpu.VMEM((width, kw), bf16),
            pltpu.VMEM((width, kw), bf16),
            pltpu.SemaphoreType.DMA((3,)),
        ],
        name="attention",
        flops=2 * total * width * (qw + 2 * kw),
    )
    ms = gather(mixed)
    hidden_own, nt, gall, gates, tgt, gates_t, tgt_t = run(
        route_kernel,
        (
            sds((micro, tok, width), f32),
            sds((total, width), bf16),
            sds((total, width), bf16),
            sds((total, 128), f32),
            sds((total, 128), f32),
            sds((experts, total), f32),
            sds((experts, total), f32),
        ),
        (ids, *xs, *ms, *gs, gain_two, router_pad, cap_pad, w_out),
        [SM] + [VM] * 15 + [HB],
        scratch=[
            pltpu.VMEM((GROUP, qw, width), bf16),
            pltpu.SemaphoreType.DMA((GROUP,)),
        ],
        name="route",
        flops=2 * total * width * width,
    )

    bits = [1 << i for i in range(dp.bit_length() - 1)]
    x_first = bits
    z_first = bits[1:] + bits[:1]

    def reduce_scatter(send, keep, order):
        got = swap(send, order[0], "dp")
        for bit in order[1:]:
            half = keep.shape[0] // 2
            send = (keep[half:].astype(f32) + got[half:].astype(f32)).astype(bf16)
            keep = (keep[:half].astype(f32) + got[:half].astype(f32)).astype(bf16)
            got = swap(send, bit, "dp")
        return keep[0].astype(f32) + got[0].astype(f32)

    big = width // dp
    small_rows = hidden_units // dp
    chunk_rows = 2 * big + 2 * small_rows
    chunk = sds((dp // 2, chunk_rows, hidden_units), bf16)
    eos, rgs, pairs, expert_sums = [], [], [], []
    for j in range(local):
        order = z_first if j == 1 else x_first
        send, keep, eo, rg, pair = run(
            functools.partial(expert_kernel, j, relative_order(dp, order)),
            (
                chunk,
                chunk,
                sds((slots, width), bf16),
                sds((slots, width), bf16),
                sds((8, total), f32),
            ),
            (ids, nt, gall, gates_t, tgt_t, w_gate, w_up, w_down),
            [SM] + [VM] * 4 + [HB] * 3,
            scratch=[
                pltpu.VMEM((width, hidden_units), bf16),
                pltpu.VMEM((width, hidden_units), bf16),
                pltpu.VMEM((hidden_units, width), bf16),
                pltpu.VMEM((width, hidden_units), f32),
                pltpu.VMEM((width, hidden_units), f32),
                pltpu.VMEM((hidden_units, width), f32),
                pltpu.SemaphoreType.DMA((3,)),
            ],
            name=f"expert{j}",
            flops=2 * slots * width * hidden_units * 12,
        )
        eos.append(eo)
        rgs.append(rg)
        pairs.append(pair)
        expert_sums.append(reduce_scatter(send, keep, order))

    row = (micro, tok, width)
    wide = (micro, tok, width + 128)
    rg0, rg2, rg_send, mix0, mix2, mix_send = run(
        combine_kernel,
        (
            sds(wide, bf16),
            sds(wide, bf16),
            sds((2, *wide), bf16),
            sds(row, bf16),
            sds(row, bf16),
            sds((2, *row), bf16),
        ),
        (ids, gates, tgt, *eos, *rgs, *pairs),
        [SM] + [VM] * 14,
        scratch=[pltpu.VMEM((128, total), f32)],
        name="combine",
        flops=2 * total * slots * width * 8,
    )
    rc, ry = scatter_sum(rg0, rg2, rg_send)
    mc, my = scatter_sum(mix0, mix2, mix_send)
    hidden_grad, branch_grad, small = run(
        hidden_kernel,
        (sds(row, f32), sds(row, bf16), sds((32, width), f32)),
        (ids, rg0, rc, ry, hidden_own, nt, gates, g_own, gain_two, router_pad),
        [SM] + [VM] * 9,
        name="hidden",
        flops=2 * micro * tok * width * 256,
    )
    bs = gather(branch_grad)
    dense_cols = 2 * qw + 2 * kw + 128
    dense_chunk = sds((dp // 2, big, dense_cols), bf16)
    send, keep, ng0, ng2, ng_send = run(
        functools.partial(backward_kernel, relative_order(dp, x_first)),
        (dense_chunk, dense_chunk, sds(row, bf16), sds(row, bf16), sds((2, *row), bf16)),
        (ids, *xs, *ms, *bs, normed, q, k, v, tabs, gain_one, small, w_query, w_key, w_value, w_out),
        [SM] + [VM] * 19 + [HB] * 4,
        scratch=[
            pltpu.VMEM((total, width), bf16),
            pltpu.VMEM((total, qw), bf16),
            pltpu.VMEM((total, qw + 2 * kw), bf16),
            pltpu.VMEM((width, qw), bf16),
            pltpu.VMEM((width, kw), bf16),
            pltpu.VMEM((width, kw), bf16),
            pltpu.VMEM((qw, width), bf16),
            pltpu.VMEM((width, dense_cols), f32),
            pltpu.VMEM((128, width), f32),
            pltpu.SemaphoreType.DMA((4,)),
        ],
        name="backward",
        flops=2 * total * width * (2 * qw + 2 * kw) * 2,
    )
    nc, ny = scatter_sum(ng0, ng2, ng_send)
    output, input_grad = run(
        final_kernel,
        (sds(row, bf16), sds(row, bf16)),
        (xs[0], ng0, nc, ny, hidden_grad, gain_one, hidden_own, mix0, mc, my),
        [VM] * 10,
        name="final",
    )
    dense = reduce_scatter(send, keep, x_first).astype(bf16)
    dense = lax.all_to_all(
        dense.reshape(GROUP, big // GROUP, dense_cols), "expert", split_axis=0, concat_axis=0, tiled=True
    )
    dense = dense.astype(f32)

    def columns(start, count):
        part = dense[:, :, start : start + count]
        return jnp.swapaxes(part, 0, 1).reshape(big // GROUP, GROUP * count)

    query_grad = columns(0, qw)
    key_grad = columns(qw, kw)
    value_grad = columns(qw + kw, kw)
    out_weight_grad = columns(qw + 2 * kw, qw)
    smalls = jnp.sum(dense[:, :, 2 * qw + 2 * kw :], axis=0)
    router_grad = smalls[:, :experts]
    norm_two_grad = smalls[:, 16]
    norm_one_grad = smalls[:, 17]
    sums = jnp.stack(expert_sums)
    gate_grad = sums[:, :big]
    up_grad = sums[:, big : 2 * big]
    down_grad = jnp.concatenate(
        [sums[:, 2 * big : 2 * big + small_rows], sums[:, 2 * big + small_rows :]], axis=-1
    )
    return (
        output[:, None],
        input_grad[:, None],
        norm_one_grad,
        norm_two_grad,
        query_grad,
        key_grad,
        value_grad,
        out_weight_grad,
        router_grad,
        gate_grad,
        up_grad,
        down_grad,
    )


def solution(mesh):
    placed = (
        P(None, "dp", "expert", None),
        P(None, "dp", "expert", None),
        P(None, "dp", "expert", None),
        P(None, "dp", "expert"),
        P(),
        P(),
        P(),
        P(),
        P(),
        P(),
        P(),
        P(),
        P("expert", None, None),
        P("expert", None, None),
        P("expert", None, None),
    )
    return jax.shard_map(
        on_device,
        mesh=mesh,
        in_specs=placed,
        out_specs=(
            P(None, "dp", "expert", None),
            P(None, "dp", "expert", None),
            P(("dp", "expert")),
            P(("dp", "expert")),
            P(("dp", "expert"), None),
            P(("dp", "expert"), None),
            P(("dp", "expert"), None),
            P(("dp", "expert"), None),
            P(("dp", "expert"), None),
            P("expert", "dp", None),
            P("expert", "dp", None),
            P("expert", "dp", None),
        ),
        check_vma=False,
    )
```
